32 devices in a mesh: grp: 4 (over y, x), node: 8 (over z, core).
Axes of the slice: x: 2, y: 2, z: 4, core: 2. Of those that a mesh axis runs over, the one named last changes fastest.
Arguments:
- coefficients: float32 [8192, 1024], P(('grp', 'node')), may hold values from -6 to 6
- transfer: float32 [5, 8192, 512], P(None, ('grp', 'node')), may hold values from -0.3125 to 0.3125
- ranks: int32 [5, 32], P(None, ('grp', 'node')), may hold values from 128 to 256, as said below
Outputs:
- applied: float32 [8192, 1024], P(('grp', 'node'))
The draws below stay inside these ranges and needn't reach their ends.
Inputs may be any that keep to these rules, and one draw needn't show every extreme that they name: `ranks`: in each level some block has rank exactly 256 and some block rank 256 // 2.
All inputs are finite; a program needn't handle non-finite values.
Results may differ from the reference program's by a relative error of at most 0.00011.
Values sent between devices are 32-bit elements; how exact they have to be, the bound alone decides.
A program may use at most 128 MiB of HBM per device.

```python
import jax
import jax.numpy as jnp
from jax import lax

K = 256
R = 1024
LEVELS = 5
BLOCKS = 32
ORDER = 8192
N_GRP = 4
N_NODE = 8


def draw_ranks(key, part):
    values = jax.random.randint(key, (LEVELS, BLOCKS), K // 2, K + 1).astype(jnp.int32)
    top_pos = jax.random.randint(jax.random.fold_in(key, 11), (LEVELS,), 0, BLOCKS)
    low_pos = (top_pos + 1 + jax.random.randint(jax.random.fold_in(key, 12), (LEVELS,), 0, BLOCKS - 1)) % BLOCKS
    level_ids = jnp.arange(LEVELS)
    values = values.at[level_ids, top_pos].set(K)
    values = values.at[level_ids, low_pos].set(K // 2)
    return values.astype(jnp.int32)


def block_scale(rng, dims, shards, least, top_value):
    def one(dim, parts):
        draws = jax.random.uniform(jax.random.fold_in(jax.random.fold_in(rng, 6), dim), (parts,), jnp.float32, least / len(shards), top_value / len(shards))
        return jnp.repeat(jnp.exp(draws), dims[dim] // parts).reshape((-1,) + (1,) * (len(dims) - dim - 1))

    level = one(*shards[0])
    for cut in shards[1:]:
        level = level * one(*cut)
    return level


def gaussian(key, dims, spread, bound, cuts=(), kind=jnp.bfloat16):
    drawn = spread * jax.random.normal(key, dims, jnp.float32)
    if cuts:
        drawn = drawn * block_scale(key, dims, cuts, -0.22, 0.18)
    return jnp.clip(drawn, -bound, bound).astype(kind)


def setup_inputs(seed: int = 0) -> dict:
    splits = jax.random.split(jax.random.key(seed), 4)
    return {
        "coefficients": gaussian(splits[0], (ORDER, R), 1.0, 6.0, ((0, 32),), jnp.float32),
        "transfer": gaussian(splits[1], (LEVELS, ORDER, 2 * K), (K * 3 // 2) ** -0.5, 0.3125, ((1, 32),), jnp.float32),
        "ranks": draw_ranks(jax.random.fold_in(splits[3], 71), 0),
    }


def reference(coefficients, transfer, ranks):
    blocks = N_GRP * N_NODE
    current = coefficients.reshape(blocks, K, R)
    row_ids = jnp.arange(K, dtype=jnp.int32)
    for level in range(LEVELS):
        span = 2 ** level
        outer = blocks // (2 * span)
        paired = current.reshape(outer, 2, span, K, R)
        stacked = jnp.concatenate([paired[:, 0], paired[:, 1]], axis=2)
        matrices = transfer[level].reshape(outer, 2, span, K, 2 * K)
        mixed = jnp.einsum("aibkm,abmr->aibkr", matrices, stacked, precision=lax.Precision.HIGHEST)
        limits = ranks[level].reshape(outer, 2, span)
        keep = row_ids[None, None, None, :] < limits[..., None]
        current = jnp.where(keep[..., None], mixed, jnp.zeros_like(mixed)).reshape(blocks, K, R)
    return current.reshape(blocks * K, R)
```

```python
import functools

import jax
import jax.numpy as jnp
from jax import lax
from jax.experimental import pallas as pl
from jax.experimental.pallas import tpu as pltpu
from jax.sharding import PartitionSpec as P

LANES = 128
UNIT = 32
EDGE = LANES // UNIT
LAGS = ((6, 6, 4), (6, 4, 4))


def split_rows(x):
    high = x.astype(jnp.bfloat16)
    low = (x - high.astype(jnp.float32)).astype(jnp.bfloat16)
    return jnp.concatenate([high, low], axis=0)


def plan(node_bits, group_bits):
    levels, due = [], (0, 0)
    for bit in range(node_bits):
        if bit:
            due = tuple(d + lag[min(bit, 2) - 1] for d, lag in zip(due, LAGS))
        levels.append(("node", bit, due))
    for bit in range(group_bits):
        due = tuple(d + lag[2] for d, lag in zip(due, LAGS))
        levels.append(("grp", bit, due))
    return levels


def kernel(
    levels, ranks_ref, coef_ref, transfer_ref, out_ref,
    raw, mats, stage, first, own, given, landed, mixed, done,
    raw_sem, stage_sem, first_send, first_recv, send_sem, recv_sem,
):
    depth, columns = coef_ref.shape
    chunks = columns // LANES
    units = columns // UNIT
    count = len(levels)

    places, partners = [], []
    for axis, bit, _ in levels:
        place = lax.axis_index(axis)
        upper = (place // 2**bit) % 2
        places.append(upper)
        partners.append({axis: place + (1 - 2 * upper) * 2**bit})
    outer = (places[1] + places[2] + 1) % 2
    dues = [inner + outer * (outside - inner) for _, _, (inner, outside) in levels]

    def cols(chunk):
        return pl.ds(pl.multiple_of(chunk * LANES, LANES), LANES)

    def load_chunk(chunk):
        return pltpu.make_async_copy(
            coef_ref.at[:, cols(chunk)], stage.at[chunk], stage_sem.at[chunk]
        )

    def load_matrix(level):
        return pltpu.make_async_copy(transfer_ref.at[level], raw.at[level], raw_sem.at[level])

    def send_first(chunk):
        return pltpu.make_async_remote_copy(
            src_ref=coef_ref.at[:, cols(chunk)],
            dst_ref=first.at[chunk],
            send_sem=first_send,
            recv_sem=first_recv.at[chunk],
            device_id=partners[0],
            device_id_type=pl.DeviceIdType.MESH,
        )

    def send(level, unit, rows):
        return pltpu.make_async_remote_copy(
            src_ref=mixed.at[level - 1, rows],
            dst_ref=landed.at[level - 1, rows],
            send_sem=send_sem.at[level - 1],
            recv_sem=recv_sem.at[level - 1, unit],
            device_id=partners[level],
            device_id_type=pl.DeviceIdType.MESH,
        )

    load_matrix(0).start()
    load_chunk(0).start()
    barrier = pltpu.get_barrier_semaphore()
    for level in range(count):
        pl.semaphore_signal(
            barrier, inc=1, device_id=partners[level], device_id_type=pl.DeviceIdType.MESH
        )
    load_chunk(1).start()
    load_matrix(1).start()
    pl.semaphore_wait(barrier, count)
    send_first(0).start()
    send_first(1).start()

    def prepare(level):
        load_matrix(level).wait()
        keep = lax.broadcasted_iota(jnp.int32, (depth, depth), 0) < ranks_ref[0, level]
        for side, place in enumerate((places[level], 1 - places[level])):
            block = raw[level, :, pl.ds(pl.multiple_of(place * depth, depth), depth)]
            both = split_rows(jnp.where(keep, block, jnp.zeros_like(block)).T)
            mats[level, 0, side * depth:(side + 1) * depth] = both[:depth]
            mats[level, 1, side * depth:(side + 1) * depth] = both[depth:]

    def mix(level, mine, other):
        total = None
        for part in range(2):
            for side, x in enumerate((mine, other)):
                term = jnp.dot(
                    x, mats[level, part, side * depth:(side + 1) * depth],
                    preferred_element_type=jnp.float32,
                )
                total = term if total is None else total + term
        half = total.shape[0] // 2
        return total[:half] + total[half:]

    def by_width(unit, body):
        inner = (unit >= EDGE) & (unit < units - EDGE)

        def run(start, width):
            start = pl.multiple_of(start, width)
            body(pl.ds(start, width), pl.ds(pl.multiple_of(2 * start, 2 * width), 2 * width))

        @pl.when(inner & (unit % 2 == 1))
        def _():
            run((unit - 1) * UNIT, 2 * UNIT)

        @pl.when(jnp.logical_not(inner))
        def _():
            run(unit * UNIT, UNIT)

    def spread(chunk, width):
        for source, target in ((stage, own), (first, given)):
            turned = source[chunk].T
            for start in range(0, LANES, width):
                where = pl.multiple_of(2 * (chunk * LANES + start), 2 * width)
                target[pl.ds(where, 2 * width)] = split_rows(turned[start:start + width])

    def open_chunk(chunk, width):
        @pl.when(chunk + 2 < chunks)
        def _():
            load_chunk(chunk + 2).start()
            send_first(chunk + 2).start()

        load_chunk(chunk).wait()
        send_first(chunk).wait_recv()
        spread(chunk, width)

    def task_first(unit):
        inner = (unit >= EDGE) & (unit < units - EDGE)

        @pl.when(inner & (unit % EDGE == 1))
        def _():
            open_chunk(unit // EDGE, 2 * UNIT)

        @pl.when(jnp.logical_not(inner) & (unit % EDGE == 0))
        def _():
            open_chunk(unit // EDGE, UNIT)

        def body(rows, twice):
            result = mix(0, own[twice], given[twice])
            mixed[0, rows] = result
            own[twice] = split_rows(result)
            send(1, unit, rows).start()

        by_width(unit, body)

    def task(level, unit):
        def body(rows, twice):
            send(level, unit, rows).wait_recv()
            result = mix(level, own[twice], split_rows(landed[level - 1, rows]))
            if level + 1 < count:
                mixed[level, rows] = result
                own[twice] = split_rows(result)
                send(level + 1, unit, rows).start()
            else:
                done[rows] = result

        by_width(unit, body)
        if level + 1 == count:
            @pl.when(unit % EDGE == EDGE - 1)
            def _():
                chunk = unit // EDGE
                out_ref[:, cols(chunk)] = done[cols(chunk)].T

    prepare(0)

    def step(s, carry):
        @pl.when(s < units)
        def _():
            task_first(s)

        @pl.when(s == 0)
        def _():
            for level in range(2, count):
                load_matrix(level).start()

        for level, due in enumerate(dues):
            if level:
                @pl.when((s >= due) & (s < due + units))
                def _():
                    task(level, s - due)

            if level + 1 < count:
                @pl.when(s == due + 1)
                def _():
                    prepare(level + 1)
        return carry

    lax.fori_loop(0, dues[-1] + units, step, 0)

    for level in range(1, count):
        pltpu.make_async_copy(
            mixed.at[level - 1], mixed.at[level - 1], send_sem.at[level - 1]
        ).wait()
    pltpu.make_async_copy(coef_ref, coef_ref, first_send).wait()


def per_device(coefficients, transfer, ranks):
    levels = plan(
        lax.axis_size("node").bit_length() - 1, lax.axis_size("grp").bit_length() - 1
    )
    count = len(levels)
    depth, columns = coefficients.shape
    chunks = columns // LANES
    units = columns // UNIT
    call = pl.pallas_call(
        functools.partial(kernel, levels),
        out_shape=jax.ShapeDtypeStruct(coefficients.shape, jnp.float32),
        in_specs=[
            pl.BlockSpec(memory_space=pltpu.SMEM),
            pl.BlockSpec(memory_space=pltpu.HBM),
            pl.BlockSpec(memory_space=pltpu.HBM),
        ],
        out_specs=pl.BlockSpec(memory_space=pltpu.VMEM),
        scratch_shapes=[
            pltpu.VMEM((count, depth, 2 * depth), jnp.float32),
            pltpu.VMEM((count, 2, 2 * depth, depth), jnp.bfloat16),
            pltpu.VMEM((chunks, depth, LANES), jnp.float32),
            pltpu.VMEM((chunks, depth, LANES), jnp.float32),
            pltpu.VMEM((2 * columns, depth), jnp.bfloat16),
            pltpu.VMEM((2 * columns, depth), jnp.bfloat16),
            pltpu.VMEM((count - 1, columns, depth), jnp.float32),
            pltpu.VMEM((count - 1, columns, depth), jnp.float32),
            pltpu.VMEM((columns, depth), jnp.float32),
            pltpu.SemaphoreType.DMA((count,)),
            pltpu.SemaphoreType.DMA((chunks,)),
            pltpu.SemaphoreType.DMA,
            pltpu.SemaphoreType.DMA((chunks,)),
            pltpu.SemaphoreType.DMA((count - 1,)),
            pltpu.SemaphoreType.DMA((count - 1, units)),
        ],
        compiler_params=pltpu.CompilerParams(
            collective_id=0, has_side_effects=True, vmem_limit_bytes=55_000_000
        ),
        name="butterfly",
    )
    return call(ranks.T, coefficients, transfer)


def solution(mesh):
    return jax.shard_map(
        per_device,
        mesh=mesh,
        in_specs=(
            P(("grp", "node"), None),
            P(None, ("grp", "node"), None),
            P(None, ("grp", "node")),
        ),
        out_specs=P(("grp", "node"), None),
        check_vma=False,
    )
```

```python
import functools

import jax
import jax.numpy as jnp
from jax import lax
from jax.experimental import pallas as pl
from jax.experimental.pallas import tpu as pltpu
from jax.sharding import PartitionSpec as P

LANES = 128
UNIT = 32
EDGE = LANES // UNIT
LAGS = ((6, 6, 4), (6, 4, 4))


def split_rows(x):
    high = x.astype(jnp.bfloat16)
    low = (x - high.astype(jnp.float32)).astype(jnp.bfloat16)
    return jnp.concatenate([high, low], axis=0)


def plan(node_bits, group_bits):
    levels, due = [], (0, 0)
    for bit in range(node_bits):
        if bit:
            due = tuple(d + lag[min(bit, 2) - 1] for d, lag in zip(due, LAGS))
        levels.append(("node", bit, due))
    for bit in range(group_bits):
        due = tuple(d + lag[2] for d, lag in zip(due, LAGS))
        levels.append(("grp", bit, due))
    return levels


def kernel(
    levels, ranks_ref, coef_ref, transfer_ref, out_ref,
    limits, raw, mats, stage, first, own, given, landed, mixed, done,
    limits_sem, raw_sem, stage_sem, first_send, first_recv, send_sem, recv_sem,
):
    depth, columns = coef_ref.shape
    units = columns // UNIT
    count = len(levels)

    places, partners = [], []
    for axis, bit, _ in levels:
        place = lax.axis_index(axis)
        upper = (place // 2**bit) % 2
        places.append(upper)
        partners.append({axis: place + (1 - 2 * upper) * 2**bit})
    outer = (places[1] + places[2] + 1) % 2
    dues = [inner + outer * (outside - inner) for _, _, (inner, outside) in levels]

    def cols(chunk):
        return pl.ds(pl.multiple_of(chunk * LANES, LANES), LANES)

    parts = [pl.ds(0, LANES), pl.ds(LANES, LANES), pl.ds(2 * LANES, columns - 2 * LANES)]

    def load_part(part):
        return pltpu.make_async_copy(
            coef_ref.at[:, parts[part]], stage.at[:, parts[part]], stage_sem.at[part]
        )

    def load_matrix(level):
        return pltpu.make_async_copy(transfer_ref.at[level], raw.at[level], raw_sem.at[level])

    def send_first(part):
        return pltpu.make_async_remote_copy(
            src_ref=coef_ref.at[:, parts[part]],
            dst_ref=first.at[:, parts[part]],
            send_sem=first_send,
            recv_sem=first_recv.at[part],
            device_id=partners[0],
            device_id_type=pl.DeviceIdType.MESH,
        )

    def slot(unit):
        late = unit // (units - EDGE)
        early = 1 - (unit + units - EDGE) // units
        narrow = early + late
        return narrow * (unit - late * (units // 2 - EDGE)) + (1 - narrow) * (EDGE // 2 + unit // 2)

    def send(level, unit, rows):
        return pltpu.make_async_remote_copy(
            src_ref=mixed.at[level - 1, rows],
            dst_ref=landed.at[level - 1, rows],
            send_sem=send_sem,
            recv_sem=recv_sem.at[level - 1, slot(unit)],
            device_id=partners[level],
            device_id_type=pl.DeviceIdType.MESH,
        )

    load_limits = pltpu.make_async_copy(ranks_ref, limits, limits_sem)
    load_limits.start()
    load_matrix(0).start()
    load_part(0).start()
    barrier = pltpu.get_barrier_semaphore()
    for level in range(count):
        pl.semaphore_signal(
            barrier, inc=1, device_id=partners[level], device_id_type=pl.DeviceIdType.MESH
        )
    load_part(1).start()
    pl.semaphore_wait(barrier, count)
    for part in range(len(parts)):
        send_first(part).start()
    load_matrix(1).start()
    load_part(2).start()

    def prepare(level):
        load_matrix(level).wait()
        keep = lax.broadcasted_iota(jnp.int32, (depth, depth), 0) < limits[0, level]
        for side, place in enumerate((places[level], 1 - places[level])):
            block = raw[level, :, pl.ds(pl.multiple_of(place * depth, depth), depth)]
            both = split_rows(jnp.where(keep, block, jnp.zeros_like(block)).T)
            mats[level, 0, side * depth:(side + 1) * depth] = both[:depth]
            mats[level, 1, side * depth:(side + 1) * depth] = both[depth:]

    def mix(level, mine, other):
        total = None
        for part in range(2):
            for side, x in enumerate((mine, other)):
                term = jnp.dot(
                    x, mats[level, part, side * depth:(side + 1) * depth],
                    preferred_element_type=jnp.float32,
                )
                total = term if total is None else total + term
        half = total.shape[0] // 2
        return total[:half] + total[half:]

    def by_width(unit, body):
        inner = (unit >= EDGE) & (unit < units - EDGE)

        def run(start, width):
            start = pl.multiple_of(start, width)
            body(pl.ds(start, width), pl.ds(pl.multiple_of(2 * start, 2 * width), 2 * width))

        @pl.when(inner & (unit % 2 == 1))
        def _():
            run((unit - 1) * UNIT, 2 * UNIT)

        @pl.when(jnp.logical_not(inner))
        def _():
            run(unit * UNIT, UNIT)

    def spread(chunk, width):
        for source, target in ((stage, own), (first, given)):
            turned = source[:, cols(chunk)].T
            for start in range(0, LANES, width):
                where = pl.multiple_of(2 * (chunk * LANES + start), 2 * width)
                target[pl.ds(where, 2 * width)] = split_rows(turned[start:start + width])

    def open_chunk(chunk, width):
        for part in range(len(parts)):
            @pl.when(chunk == part)
            def _():
                load_part(part).wait()
                send_first(part).wait_recv()

        spread(chunk, width)

    def task_first(unit):
        inner = (unit >= EDGE) & (unit < units - EDGE)

        @pl.when(inner & (unit % EDGE == 1))
        def _():
            open_chunk(unit // EDGE, 2 * UNIT)

        @pl.when(jnp.logical_not(inner) & (unit % EDGE == 0))
        def _():
            open_chunk(unit // EDGE, UNIT)

        def body(rows, twice):
            result = mix(0, own[twice], given[twice])
            mixed[0, rows] = result
            own[twice] = split_rows(result)
            send(1, unit, rows).start()

        by_width(unit, body)

    def task(level, unit):
        def body(rows, twice):
            send(level, unit, rows).wait_recv()
            result = mix(level, own[twice], split_rows(landed[level - 1, rows]))
            if level + 1 < count:
                mixed[level, rows] = result
                own[twice] = split_rows(result)
                send(level + 1, unit, rows).start()
            else:
                done[rows] = result

        by_width(unit, body)
        if level + 1 == count:
            @pl.when(unit % EDGE == EDGE - 1)
            def _():
                chunk = unit // EDGE
                out_ref[:, cols(chunk)] = done[cols(chunk)].T

    load_limits.wait()
    prepare(0)

    def step(s, carry):
        @pl.when(s < units)
        def _():
            task_first(s)

        @pl.when(s == 0)
        def _():
            for level in range(2, count):
                load_matrix(level).start()

        for level, due in enumerate(dues):
            if level:
                @pl.when((s >= due) & (s < due + units))
                def _():
                    task(level, s - due)

            if level + 1 < count:
                @pl.when(s == due + 1)
                def _():
                    prepare(level + 1)
        return carry

    lax.fori_loop(0, dues[-1] + units, step, 0)

    pltpu.make_async_copy(mixed, mixed, send_sem).wait()
    pltpu.make_async_copy(coef_ref, coef_ref, first_send).wait()


def per_device(coefficients, transfer, ranks):
    levels = plan(
        lax.axis_size("node").bit_length() - 1, lax.axis_size("grp").bit_length() - 1
    )
    count = len(levels)
    depth, columns = coefficients.shape
    units = columns // UNIT
    call = pl.pallas_call(
        functools.partial(kernel, levels),
        out_shape=jax.ShapeDtypeStruct(coefficients.shape, jnp.float32),
        in_specs=[
            pl.BlockSpec(memory_space=pltpu.HBM),
            pl.BlockSpec(memory_space=pltpu.HBM),
            pl.BlockSpec(memory_space=pltpu.HBM),
        ],
        out_specs=pl.BlockSpec(memory_space=pltpu.VMEM),
        scratch_shapes=[
            pltpu.SMEM((1, count), jnp.int32),
            pltpu.VMEM((count, depth, 2 * depth), jnp.float32),
            pltpu.VMEM((count, 2, 2 * depth, depth), jnp.bfloat16),
            pltpu.VMEM((depth, columns), jnp.float32),
            pltpu.VMEM((depth, columns), jnp.float32),
            pltpu.VMEM((2 * columns, depth), jnp.bfloat16),
            pltpu.VMEM((2 * columns, depth), jnp.bfloat16),
            pltpu.VMEM((count - 1, columns, depth), jnp.float32),
            pltpu.VMEM((count - 1, columns, depth), jnp.float32),
            pltpu.VMEM((columns, depth), jnp.float32),
            pltpu.SemaphoreType.DMA,
            pltpu.SemaphoreType.DMA((count,)),
            pltpu.SemaphoreType.DMA((3,)),
            pltpu.SemaphoreType.DMA,
            pltpu.SemaphoreType.DMA((3,)),
            pltpu.SemaphoreType.DMA,
            pltpu.SemaphoreType.DMA((count - 1, units // 2 + EDGE)),
        ],
        compiler_params=pltpu.CompilerParams(
            collective_id=0, has_side_effects=True, vmem_limit_bytes=55_000_000
        ),
        name="butterfly",
    )
    return call(pltpu.with_memory_space_constraint(ranks.T, pltpu.HBM), coefficients, transfer)


def solution(mesh):
    return jax.shard_map(
        per_device,
        mesh=mesh,
        in_specs=(
            P(("grp", "node"), None),
            P(None, ("grp", "node"), None),
            P(None, ("grp", "node")),
        ),
        out_specs=P(("grp", "node"), None),
        check_vma=False,
    )
```

```python
import functools

import jax
import jax.numpy as jnp
from jax import lax
from jax.experimental import pallas as pl
from jax.experimental.pallas import tpu as pltpu
from jax.sharding import PartitionSpec as P

LANES = 128
UNIT = 32
EDGE = LANES // UNIT
TURN = 10
LAGS = ((6, 6, 4), (6, 4, 4))


def split_rows(x):
    high = x.astype(jnp.bfloat16)
    low = (x - high.astype(jnp.float32)).astype(jnp.bfloat16)
    return jnp.concatenate([high, low], axis=0)


def plan(node_bits, group_bits):
    levels, due = [], (0, 0)
    for bit in range(node_bits):
        if bit:
            due = tuple(d + lag[min(bit, 2) - 1] for d, lag in zip(due, LAGS))
        levels.append(("node", bit, due))
    for bit in range(group_bits):
        due = tuple(d + lag[2] for d, lag in zip(due, LAGS))
        levels.append(("grp", bit, due))
    return levels


def kernel(
    levels, ranks_ref, coef_ref, transfer_ref, out_ref,
    limits, raw, mats, stage, first, own, given, landed, mixed, done,
    limits_sem, raw_sem, stage_sem, first_send, first_recv, send_sem, recv_sem,
):
    depth, columns = coef_ref.shape
    units = columns // UNIT
    count = len(levels)

    places, partners = [], []
    for axis, bit, _ in levels:
        place = lax.axis_index(axis)
        upper = (place // 2**bit) % 2
        places.append(upper)
        partners.append({axis: place + (1 - 2 * upper) * 2**bit})
    outer = (places[1] + places[2] + 1) % 2
    dues = [inner + outer * (outside - inner) for _, _, (inner, outside) in levels]

    def cols(chunk):
        return pl.ds(pl.multiple_of(chunk * LANES, LANES), LANES)

    parts = [pl.ds(0, LANES), pl.ds(LANES, LANES), pl.ds(2 * LANES, columns - 2 * LANES)]

    def load_part(part):
        return pltpu.make_async_copy(
            coef_ref.at[:, parts[part]], stage.at[:, parts[part]], stage_sem.at[part]
        )

    def load_matrix(level):
        return pltpu.make_async_copy(transfer_ref.at[level], raw.at[level], raw_sem.at[level])

    later = pl.ds(2, count - 2)
    load_later = pltpu.make_async_copy(transfer_ref.at[later], raw.at[later], raw_sem.at[2])

    def send_first(part):
        return pltpu.make_async_remote_copy(
            src_ref=coef_ref.at[:, parts[part]],
            dst_ref=first.at[:, parts[part]],
            send_sem=first_send,
            recv_sem=first_recv.at[part],
            device_id=partners[0],
            device_id_type=pl.DeviceIdType.MESH,
        )

    def slot(unit):
        late = unit // (units - EDGE)
        early = 1 - (unit + units - EDGE) // units
        narrow = early + late
        return narrow * (unit - late * (units // 2 - EDGE)) + (1 - narrow) * (EDGE // 2 + unit // 2)

    def send(level, unit, rows):
        return pltpu.make_async_remote_copy(
            src_ref=mixed.at[level - 1, rows],
            dst_ref=landed.at[level - 1, rows],
            send_sem=send_sem,
            recv_sem=recv_sem.at[level - 1, slot(unit) % TURN],
            device_id=partners[level],
            device_id_type=pl.DeviceIdType.MESH,
        )

    load_limits = pltpu.make_async_copy(ranks_ref, limits, limits_sem)
    load_limits.start()
    load_matrix(0).start()
    load_part(0).start()
    barrier = pltpu.get_barrier_semaphore()
    for level in range(count):
        pl.semaphore_signal(
            barrier, inc=1, device_id=partners[level], device_id_type=pl.DeviceIdType.MESH
        )
    load_part(1).start()
    pl.semaphore_wait(barrier, count)
    for part in range(len(parts)):
        send_first(part).start()
    load_matrix(1).start()
    load_part(2).start()

    def prepare(level):
        if level < 2:
            load_matrix(level).wait()
        elif level == 2:
            load_later.wait()
        keep = lax.broadcasted_iota(jnp.int32, (depth, depth), 0) < limits[0, level]
        for side, place in enumerate((places[level], 1 - places[level])):
            block = raw[level, :, pl.ds(pl.multiple_of(place * depth, depth), depth)]
            both = split_rows(jnp.where(keep, block, jnp.zeros_like(block)).T)
            mats[level, 0, side * depth:(side + 1) * depth] = both[:depth]
            mats[level, 1, side * depth:(side + 1) * depth] = both[depth:]

    def mix(level, mine, other):
        total = None
        for part in range(2):
            for side, x in enumerate((mine, other)):
                term = jnp.dot(
                    x, mats[level, part, side * depth:(side + 1) * depth],
                    preferred_element_type=jnp.float32,
                )
                total = term if total is None else total + term
        half = total.shape[0] // 2
        return total[:half] + total[half:]

    def by_width(unit, body):
        inner = (unit >= EDGE) & (unit < units - EDGE)

        def run(start, width):
            start = pl.multiple_of(start, width)
            body(pl.ds(start, width), pl.ds(pl.multiple_of(2 * start, 2 * width), 2 * width))

        @pl.when(inner & (unit % 2 == 1))
        def _():
            run((unit - 1) * UNIT, 2 * UNIT)

        @pl.when(jnp.logical_not(inner))
        def _():
            run(unit * UNIT, UNIT)

    def spread(chunk, width):
        for source, target in ((stage, own), (first, given)):
            turned = source[:, cols(chunk)].T
            for start in range(0, LANES, width):
                where = pl.multiple_of(2 * (chunk * LANES + start), 2 * width)
                target[pl.ds(where, 2 * width)] = split_rows(turned[start:start + width])

    def open_chunk(chunk, width):
        for part in range(len(parts)):
            @pl.when(chunk == part)
            def _():
                load_part(part).wait()
                send_first(part).wait_recv()

        spread(chunk, width)

    def task_first(unit):
        inner = (unit >= EDGE) & (unit < units - EDGE)

        @pl.when(inner & (unit % EDGE == 1))
        def _():
            open_chunk(unit // EDGE, 2 * UNIT)

        @pl.when(jnp.logical_not(inner) & (unit % EDGE == 0))
        def _():
            open_chunk(unit // EDGE, UNIT)

        def body(rows, twice):
            result = mix(0, own[twice], given[twice])
            mixed[0, rows] = result
            own[twice] = split_rows(result)
            send(1, unit, rows).start()

        by_width(unit, body)

    def task(level, unit):
        def body(rows, twice):
            send(level, unit, rows).wait_recv()
            result = mix(level, own[twice], split_rows(landed[level - 1, rows]))
            if level + 1 < count:
                mixed[level, rows] = result
                own[twice] = split_rows(result)
                send(level + 1, unit, rows).start()
            else:
                done[rows] = result

        by_width(unit, body)
        if level + 1 == count:
            @pl.when(unit % EDGE == EDGE - 1)
            def _():
                chunk = unit // EDGE
                out_ref[:, cols(chunk)] = done[cols(chunk)].T

    load_limits.wait()
    prepare(0)

    def step(s, carry):
        @pl.when(s < units)
        def _():
            task_first(s)

        @pl.when(s == 0)
        def _():
            load_later.start()

        for level, due in enumerate(dues):
            if level:
                @pl.when((s >= due) & (s < due + units))
                def _():
                    task(level, s - due)

            if level + 1 < count:
                @pl.when(s == due + 1)
                def _():
                    prepare(level + 1)
        return carry

    lax.fori_loop(0, dues[-1] + units, step, 0)

    pltpu.make_async_copy(mixed, mixed, send_sem).wait()
    pltpu.make_async_copy(coef_ref, coef_ref, first_send).wait()


def per_device(coefficients, transfer, ranks):
    levels = plan(
        lax.axis_size("node").bit_length() - 1, lax.axis_size("grp").bit_length() - 1
    )
    count = len(levels)
    depth, columns = coefficients.shape
    units = columns // UNIT
    call = pl.pallas_call(
        functools.partial(kernel, levels),
        out_shape=jax.ShapeDtypeStruct(coefficients.shape, jnp.float32),
        in_specs=[
            pl.BlockSpec(memory_space=pltpu.HBM),
            pl.BlockSpec(memory_space=pltpu.HBM),
            pl.BlockSpec(memory_space=pltpu.HBM),
        ],
        out_specs=pl.BlockSpec(memory_space=pltpu.VMEM),
        scratch_shapes=[
            pltpu.SMEM((1, count), jnp.int32),
            pltpu.VMEM((count, depth, 2 * depth), jnp.float32),
            pltpu.VMEM((count, 2, 2 * depth, depth), jnp.bfloat16),
            pltpu.VMEM((depth, columns), jnp.float32),
            pltpu.VMEM((depth, columns), jnp.float32),
            pltpu.VMEM((2 * columns, depth), jnp.bfloat16),
            pltpu.VMEM((2 * columns, depth), jnp.bfloat16),
            pltpu.VMEM((count - 1, columns, depth), jnp.float32),
            pltpu.VMEM((count - 1, columns, depth), jnp.float32),
            pltpu.VMEM((columns, depth), jnp.float32),
            pltpu.SemaphoreType.DMA,
            pltpu.SemaphoreType.DMA((3,)),
            pltpu.SemaphoreType.DMA((3,)),
            pltpu.SemaphoreType.DMA,
            pltpu.SemaphoreType.DMA((3,)),
            pltpu.SemaphoreType.DMA,
            pltpu.SemaphoreType.DMA((count - 1, TURN)),
        ],
        compiler_params=pltpu.CompilerParams(
            collective_id=0, has_side_effects=True, vmem_limit_bytes=55_000_000
        ),
        name="butterfly",
    )
    return call(pltpu.with_memory_space_constraint(ranks.T, pltpu.HBM), coefficients, transfer)


def solution(mesh):
    return jax.shard_map(
        per_device,
        mesh=mesh,
        in_specs=(
            P(("grp", "node"), None),
            P(None, ("grp", "node"), None),
            P(None, ("grp", "node")),
        ),
        out_specs=P(("grp", "node"), None),
        check_vma=False,
    )
```

```python
import functools

import jax
import jax.numpy as jnp
from jax import lax
from jax.experimental import pallas as pl
from jax.experimental.pallas import tpu as pltpu
from jax.sharding import PartitionSpec as P

LANES = 128
UNIT = 32
EDGE = LANES // UNIT
HELD, HOLD = 3, 3
TURN = 10
LAGS = ((6, 6, 4), (6, 4, 4))


def split_rows(x):
    high = x.astype(jnp.bfloat16)
    low = (x - high.astype(jnp.float32)).astype(jnp.bfloat16)
    return jnp.concatenate([high, low], axis=0)


def plan(node_bits, group_bits):
    levels, due = [], (0, 0)
    for bit in range(node_bits):
        if bit:
            due = tuple(d + lag[min(bit, 2) - 1] for d, lag in zip(due, LAGS))
        levels.append(("node", bit, due))
    for bit in range(group_bits):
        due = tuple(d + lag[2] for d, lag in zip(due, LAGS))
        levels.append(("grp", bit, due))
    return levels


def kernel(
    levels, ranks_ref, coef_ref, transfer_ref, out_ref,
    limits, raw, mats, stage, first, own, given, landed, mixed, done,
    limits_sem, raw_sem, stage_sem, first_send, first_recv, send_sem, recv_sem,
):
    depth, columns = coef_ref.shape
    units = columns // UNIT
    count = len(levels)

    places, partners = [], []
    for axis, bit, _ in levels:
        place = lax.axis_index(axis)
        upper = (place // 2**bit) % 2
        places.append(upper)
        partners.append({axis: place + (1 - 2 * upper) * 2**bit})
    outer = (places[1] + places[2] + 1) % 2
    hold = HOLD * outer
    dues = [inner + outer * (outside - inner) for _, _, (inner, outside) in levels]

    def cols(chunk):
        return pl.ds(pl.multiple_of(chunk * LANES, LANES), LANES)

    parts = [pl.ds(0, LANES), pl.ds(LANES, LANES), pl.ds(2 * LANES, columns - 2 * LANES)]

    def load_part(part):
        return pltpu.make_async_copy(
            coef_ref.at[:, parts[part]], stage.at[:, parts[part]], stage_sem.at[part]
        )

    def load_matrix(level):
        return pltpu.make_async_copy(transfer_ref.at[level], raw.at[level], raw_sem.at[level])

    later = pl.ds(2, count - 2)
    load_later = pltpu.make_async_copy(transfer_ref.at[later], raw.at[later], raw_sem.at[2])

    def send_first(part):
        return pltpu.make_async_remote_copy(
            src_ref=coef_ref.at[:, parts[part]],
            dst_ref=first.at[:, parts[part]],
            send_sem=first_send,
            recv_sem=first_recv.at[part],
            device_id=partners[0],
            device_id_type=pl.DeviceIdType.MESH,
        )

    def slot(unit):
        late = unit // (units - EDGE)
        early = 1 - (unit + units - EDGE) // units
        narrow = early + late
        return narrow * (unit - late * (units // 2 - EDGE)) + (1 - narrow) * (EDGE // 2 + unit // 2)

    def send(level, unit, rows):
        return pltpu.make_async_remote_copy(
            src_ref=mixed.at[level - 1, rows],
            dst_ref=landed.at[level - 1, rows],
            send_sem=send_sem,
            recv_sem=recv_sem.at[level - 1, slot(unit) % TURN],
            device_id=partners[level],
            device_id_type=pl.DeviceIdType.MESH,
        )

    load_limits = pltpu.make_async_copy(ranks_ref, limits, limits_sem)
    load_limits.start()
    load_matrix(0).start()
    load_part(0).start()
    barrier = pltpu.get_barrier_semaphore()
    for level in range(count):
        pl.semaphore_signal(
            barrier, inc=1, device_id=partners[level], device_id_type=pl.DeviceIdType.MESH
        )
    load_part(1).start()
    pl.semaphore_wait(barrier, count)
    for part in range(len(parts)):
        send_first(part).start()
    load_matrix(1).start()
    load_part(2).start()

    def prepare(level):
        if level < 2:
            load_matrix(level).wait()
        elif level == 2:
            load_later.wait()
        keep = lax.broadcasted_iota(jnp.int32, (depth, depth), 0) < limits[0, level]
        for side, place in enumerate((places[level], 1 - places[level])):
            block = raw[level, :, pl.ds(pl.multiple_of(place * depth, depth), depth)]
            both = split_rows(jnp.where(keep, block, jnp.zeros_like(block)).T)
            mats[level, 0, side * depth:(side + 1) * depth] = both[:depth]
            mats[level, 1, side * depth:(side + 1) * depth] = both[depth:]

    def mix(level, mine, other):
        total = None
        for part in range(2):
            for side, x in enumerate((mine, other)):
                term = jnp.dot(
                    x, mats[level, part, side * depth:(side + 1) * depth],
                    preferred_element_type=jnp.float32,
                )
                total = term if total is None else total + term
        half = total.shape[0] // 2
        return total[:half] + total[half:]

    def by_width(unit, body):
        inner = (unit >= EDGE) & (unit < units - EDGE)

        def run(start, width):
            start = pl.multiple_of(start, width)
            body(pl.ds(start, width), pl.ds(pl.multiple_of(2 * start, 2 * width), 2 * width))

        @pl.when(inner & (unit % 2 == 1))
        def _():
            run((unit - 1) * UNIT, 2 * UNIT)

        @pl.when(jnp.logical_not(inner))
        def _():
            run(unit * UNIT, UNIT)

    def spread(chunk, width):
        for source, target in ((stage, own), (first, given)):
            turned = source[:, cols(chunk)].T
            for start in range(0, LANES, width):
                where = pl.multiple_of(2 * (chunk * LANES + start), 2 * width)
                target[pl.ds(where, 2 * width)] = split_rows(turned[start:start + width])

    def open_chunk(chunk, width):
        for part in range(len(parts)):
            @pl.when(chunk == part)
            def _():
                load_part(part).wait()
                send_first(part).wait_recv()

        spread(chunk, width)

    def task_first(unit):
        inner = (unit >= EDGE) & (unit < units - EDGE)

        @pl.when(inner & (unit % EDGE == 1))
        def _():
            open_chunk(unit // EDGE, 2 * UNIT)

        @pl.when(jnp.logical_not(inner) & (unit % EDGE == 0))
        def _():
            open_chunk(unit // EDGE, UNIT)

        def body(rows, twice):
            result = mix(0, own[twice], given[twice])
            mixed[0, rows] = result
            own[twice] = split_rows(result)
            send(1, unit, rows).start()

        by_width(unit, body)

    def task(level, unit):
        def body(rows, twice):
            send(level, unit, rows).wait_recv()
            result = mix(level, own[twice], split_rows(landed[level - 1, rows]))
            if level + 1 < count:
                mixed[level, rows] = result
                own[twice] = split_rows(result)
                send(level + 1, unit, rows).start()
            else:
                done[rows] = result

        by_width(unit, body)
        if level + 1 == count:
            @pl.when(unit % EDGE == EDGE - 1)
            def _():
                chunk = unit // EDGE
                out_ref[:, cols(chunk)] = done[cols(chunk)].T

    load_limits.wait()
    prepare(0)

    def step(s, carry):
        @pl.when(s < units)
        def _():
            task_first(s)

        @pl.when(s == 0)
        def _():
            load_later.start()

        for level, due in enumerate(dues):
            if level == 1:
                at = s - due
                late = at // (units - HELD + hold)

                @pl.when((at >= 0) & (at < units + hold) & ((at < units - HELD) | (late > 0)))
                def _():
                    task(1, at - late * hold)

            elif level:
                @pl.when((s >= due) & (s < due + units))
                def _():
                    task(level, s - due)

            if level + 1 < count:
                @pl.when(s == due + 1)
                def _():
                    prepare(level + 1)
        return carry

    lax.fori_loop(0, dues[-1] + units, step, 0)

    pltpu.make_async_copy(mixed, mixed, send_sem).wait()
    pltpu.make_async_copy(coef_ref, coef_ref, first_send).wait()


def per_device(coefficients, transfer, ranks):
    levels = plan(
        lax.axis_size("node").bit_length() - 1, lax.axis_size("grp").bit_length() - 1
    )
    count = len(levels)
    depth, columns = coefficients.shape
    units = columns // UNIT
    call = pl.pallas_call(
        functools.partial(kernel, levels),
        out_shape=jax.ShapeDtypeStruct(coefficients.shape, jnp.float32),
        in_specs=[
            pl.BlockSpec(memory_space=pltpu.HBM),
            pl.BlockSpec(memory_space=pltpu.HBM),
            pl.BlockSpec(memory_space=pltpu.HBM),
        ],
        out_specs=pl.BlockSpec(memory_space=pltpu.VMEM),
        scratch_shapes=[
            pltpu.SMEM((1, count), jnp.int32),
            pltpu.VMEM((count, depth, 2 * depth), jnp.float32),
            pltpu.VMEM((count, 2, 2 * depth, depth), jnp.bfloat16),
            pltpu.VMEM((depth, columns), jnp.float32),
            pltpu.VMEM((depth, columns), jnp.float32),
            pltpu.VMEM((2 * columns, depth), jnp.bfloat16),
            pltpu.VMEM((2 * columns, depth), jnp.bfloat16),
            pltpu.VMEM((count - 1, columns, depth), jnp.float32),
            pltpu.VMEM((count - 1, columns, depth), jnp.float32),
            pltpu.VMEM((columns, depth), jnp.float32),
            pltpu.SemaphoreType.DMA,
            pltpu.SemaphoreType.DMA((3,)),
            pltpu.SemaphoreType.DMA((3,)),
            pltpu.SemaphoreType.DMA,
            pltpu.SemaphoreType.DMA((3,)),
            pltpu.SemaphoreType.DMA,
            pltpu.SemaphoreType.DMA((count - 1, TURN)),
        ],
        compiler_params=pltpu.CompilerParams(
            collective_id=0, has_side_effects=True, vmem_limit_bytes=55_000_000
        ),
        name="butterfly",
    )
    return call(pltpu.with_memory_space_constraint(ranks.T, pltpu.HBM), coefficients, transfer)


def solution(mesh):
    return jax.shard_map(
        per_device,
        mesh=mesh,
        in_specs=(
            P(("grp", "node"), None),
            P(None, ("grp", "node"), None),
            P(None, ("grp", "node")),
        ),
        out_specs=P(("grp", "node"), None),
        check_vma=False,
    )
```

```python
import functools

import jax
import jax.numpy as jnp
from jax import lax
from jax.experimental import pallas as pl
from jax.experimental.pallas import tpu as pltpu
from jax.sharding import PartitionSpec as P

LANES = 128
UNIT = 32
EDGE = LANES // UNIT
HELD, HOLD = 3, 3
TURN = 10
LAGS = ((4, 6, 4), (6, 4, 4))


def split_rows(x):
    high = x.astype(jnp.bfloat16)
    low = (x - high.astype(jnp.float32)).astype(jnp.bfloat16)
    return jnp.concatenate([high, low], axis=0)


def plan(node_bits, group_bits):
    levels, due = [], (0, 0)
    for bit in range(node_bits):
        if bit:
            due = tuple(d + lag[min(bit, 2) - 1] for d, lag in zip(due, LAGS))
        levels.append(("node", bit, due))
    for bit in range(group_bits):
        due = tuple(d + lag[2] for d, lag in zip(due, LAGS))
        levels.append(("grp", bit, due))
    return levels


def kernel(
    levels, ranks_ref, coef_ref, transfer_ref, out_ref,
    limits, raw, mats, stage, first, own, given, landed, mixed, done,
    limits_sem, raw_sem, stage_sem, first_send, first_recv, send_sem, recv_sem,
):
    depth, columns = coef_ref.shape
    units = columns // UNIT
    count = len(levels)

    places, partners = [], []
    for axis, bit, _ in levels:
        place = lax.axis_index(axis)
        upper = (place // 2**bit) % 2
        places.append(upper)
        partners.append({axis: place + (1 - 2 * upper) * 2**bit})
    outer = (places[1] + places[2] + 1) % 2
    hold = HOLD * outer
    dues = [inner + outer * (outside - inner) for _, _, (inner, outside) in levels]

    def cols(chunk):
        return pl.ds(pl.multiple_of(chunk * LANES, LANES), LANES)

    parts = [pl.ds(0, LANES), pl.ds(LANES, LANES), pl.ds(2 * LANES, columns - 2 * LANES)]

    def load_part(part):
        return pltpu.make_async_copy(
            coef_ref.at[:, parts[part]], stage.at[:, parts[part]], stage_sem.at[part]
        )

    def load_matrix(level):
        return pltpu.make_async_copy(transfer_ref.at[level], raw.at[level], raw_sem.at[level])

    later = pl.ds(2, count - 2)
    load_later = pltpu.make_async_copy(transfer_ref.at[later], raw.at[later], raw_sem.at[2])

    def send_first(part):
        return pltpu.make_async_remote_copy(
            src_ref=coef_ref.at[:, parts[part]],
            dst_ref=first.at[:, parts[part]],
            send_sem=first_send,
            recv_sem=first_recv.at[part],
            device_id=partners[0],
            device_id_type=pl.DeviceIdType.MESH,
        )

    def slot(unit):
        late = unit // (units - EDGE)
        early = 1 - (unit + units - EDGE) // units
        narrow = early + late
        return narrow * (unit - late * (units // 2 - EDGE)) + (1 - narrow) * (EDGE // 2 + unit // 2)

    def send(level, unit, rows):
        return pltpu.make_async_remote_copy(
            src_ref=mixed.at[level - 1, rows],
            dst_ref=landed.at[level - 1, rows],
            send_sem=send_sem,
            recv_sem=recv_sem.at[level - 1, slot(unit) % TURN],
            device_id=partners[level],
            device_id_type=pl.DeviceIdType.MESH,
        )

    load_limits = pltpu.make_async_copy(ranks_ref, limits, limits_sem)
    load_limits.start()
    load_matrix(0).start()
    load_part(0).start()
    barrier = pltpu.get_barrier_semaphore()
    for level in range(count):
        pl.semaphore_signal(
            barrier, inc=1, device_id=partners[level], device_id_type=pl.DeviceIdType.MESH
        )
    load_part(1).start()
    pl.semaphore_wait(barrier, count)
    for part in range(len(parts)):
        send_first(part).start()
    load_matrix(1).start()
    load_part(2).start()

    def prepare(level):
        if level < 2:
            load_matrix(level).wait()
        elif level == 2:
            load_later.wait()
        keep = lax.broadcasted_iota(jnp.int32, (depth, depth), 0) < limits[0, level]
        for side, place in enumerate((places[level], 1 - places[level])):
            block = raw[level, :, pl.ds(pl.multiple_of(place * depth, depth), depth)]
            both = split_rows(jnp.where(keep, block, jnp.zeros_like(block)).T)
            mats[level, 0, side * depth:(side + 1) * depth] = both[:depth]
            mats[level, 1, side * depth:(side + 1) * depth] = both[depth:]

    def mix(level, mine, other):
        total = None
        for part in range(2):
            for side, x in enumerate((mine, other)):
                term = jnp.dot(
                    x, mats[level, part, side * depth:(side + 1) * depth],
                    preferred_element_type=jnp.float32,
                )
                total = term if total is None else total + term
        half = total.shape[0] // 2
        return total[:half] + total[half:]

    def by_width(unit, body):
        inner = (unit >= EDGE) & (unit < units - EDGE)

        def run(start, width):
            start = pl.multiple_of(start, width)
            body(pl.ds(start, width), pl.ds(pl.multiple_of(2 * start, 2 * width), 2 * width))

        @pl.when(inner & (unit % 2 == 1))
        def _():
            run((unit - 1) * UNIT, 2 * UNIT)

        @pl.when(jnp.logical_not(inner))
        def _():
            run(unit * UNIT, UNIT)

    def spread(chunk, width):
        for source, target in ((stage, own), (first, given)):
            turned = source[:, cols(chunk)].T
            for start in range(0, LANES, width):
                where = pl.multiple_of(2 * (chunk * LANES + start), 2 * width)
                target[pl.ds(where, 2 * width)] = split_rows(turned[start:start + width])

    def open_chunk(chunk, width):
        for part in range(len(parts)):
            @pl.when(chunk == part)
            def _():
                load_part(part).wait()
                send_first(part).wait_recv()

        spread(chunk, width)

    def task_first(unit):
        inner = (unit >= EDGE) & (unit < units - EDGE)

        @pl.when(inner & (unit % EDGE == 1))
        def _():
            open_chunk(unit // EDGE, 2 * UNIT)

        @pl.when(jnp.logical_not(inner) & (unit % EDGE == 0))
        def _():
            open_chunk(unit // EDGE, UNIT)

        def body(rows, twice):
            result = mix(0, own[twice], given[twice])
            mixed[0, rows] = result
            own[twice] = split_rows(result)
            send(1, unit, rows).start()

        by_width(unit, body)

    def task(level, unit):
        def body(rows, twice):
            send(level, unit, rows).wait_recv()
            result = mix(level, own[twice], split_rows(landed[level - 1, rows]))
            if level + 1 < count:
                mixed[level, rows] = result
                own[twice] = split_rows(result)
                send(level + 1, unit, rows).start()
            else:
                done[rows] = result

        by_width(unit, body)
        if level + 1 == count:
            @pl.when(unit % EDGE == EDGE - 1)
            def _():
                chunk = unit // EDGE
                out_ref[:, cols(chunk)] = done[cols(chunk)].T

    load_limits.wait()
    prepare(0)

    def step(s, carry):
        @pl.when(s < units)
        def _():
            task_first(s)

        @pl.when(s == 0)
        def _():
            load_later.start()

        for level, due in enumerate(dues):
            if level == 1:
                at = s - due
                late = at // (units - HELD + hold)

                @pl.when((at >= 0) & (at < units + hold) & ((at < units - HELD) | (late > 0)))
                def _():
                    task(1, at - late * hold)

            elif level:
                @pl.when((s >= due) & (s < due + units))
                def _():
                    task(level, s - due)

            if level + 1 < count:
                @pl.when(s == due + 1)
                def _():
                    prepare(level + 1)
        return carry

    lax.fori_loop(0, dues[-1] + units, step, 0)

    pltpu.make_async_copy(mixed, mixed, send_sem).wait()
    pltpu.make_async_copy(coef_ref, coef_ref, first_send).wait()


def per_device(coefficients, transfer, ranks):
    levels = plan(
        lax.axis_size("node").bit_length() - 1, lax.axis_size("grp").bit_length() - 1
    )
    count = len(levels)
    depth, columns = coefficients.shape
    units = columns // UNIT
    call = pl.pallas_call(
        functools.partial(kernel, levels),
        out_shape=jax.ShapeDtypeStruct(coefficients.shape, jnp.float32),
        in_specs=[
            pl.BlockSpec(memory_space=pltpu.HBM),
            pl.BlockSpec(memory_space=pltpu.HBM),
            pl.BlockSpec(memory_space=pltpu.HBM),
        ],
        out_specs=pl.BlockSpec(memory_space=pltpu.VMEM),
        scratch_shapes=[
            pltpu.SMEM((1, count), jnp.int32),
            pltpu.VMEM((count, depth, 2 * depth), jnp.float32),
            pltpu.VMEM((count, 2, 2 * depth, depth), jnp.bfloat16),
            pltpu.VMEM((depth, columns), jnp.float32),
            pltpu.VMEM((depth, columns), jnp.float32),
            pltpu.VMEM((2 * columns, depth), jnp.bfloat16),
            pltpu.VMEM((2 * columns, depth), jnp.bfloat16),
            pltpu.VMEM((count - 1, columns, depth), jnp.float32),
            pltpu.VMEM((count - 1, columns, depth), jnp.float32),
            pltpu.VMEM((columns, depth), jnp.float32),
            pltpu.SemaphoreType.DMA,
            pltpu.SemaphoreType.DMA((3,)),
            pltpu.SemaphoreType.DMA((3,)),
            pltpu.SemaphoreType.DMA,
            pltpu.SemaphoreType.DMA((3,)),
            pltpu.SemaphoreType.DMA,
            pltpu.SemaphoreType.DMA((count - 1, TURN)),
        ],
        compiler_params=pltpu.CompilerParams(
            collective_id=0, has_side_effects=True, vmem_limit_bytes=55_000_000
        ),
        name="butterfly",
    )
    return call(pltpu.with_memory_space_constraint(ranks.T, pltpu.HBM), coefficients, transfer)


def solution(mesh):
    return jax.shard_map(
        per_device,
        mesh=mesh,
        in_specs=(
            P(("grp", "node"), None),
            P(None, ("grp", "node"), None),
            P(None, ("grp", "node")),
        ),
        out_specs=P(("grp", "node"), None),
        check_vma=False,
    )
```

```python
import functools

import jax
import jax.numpy as jnp
from jax import lax
from jax.experimental import pallas as pl
from jax.experimental.pallas import tpu as pltpu
from jax.sharding import PartitionSpec as P

LANES = 128
UNIT = 32
EDGE = LANES // UNIT
HELD, HOLD = 3, 3
TURN = 10
LAGS = ((4, 6, 3), (6, 4, 4))


def split_rows(x):
    high = x.astype(jnp.bfloat16)
    low = (x - high.astype(jnp.float32)).astype(jnp.bfloat16)
    return jnp.concatenate([high, low], axis=0)


def plan(node_bits, group_bits):
    levels, due = [], (0, 0)
    for bit in range(node_bits):
        if bit:
            due = tuple(d + lag[min(bit, 2) - 1] for d, lag in zip(due, LAGS))
        levels.append(("node", bit, due))
    for bit in range(group_bits):
        due = tuple(d + lag[2] for d, lag in zip(due, LAGS))
        levels.append(("grp", bit, due))
    return levels


def kernel(
    levels, ranks_ref, coef_ref, transfer_ref, out_ref,
    limits, raw, mats, stage, first, own, given, landed, mixed, done,
    limits_sem, raw_sem, stage_sem, first_send, first_recv, send_sem, recv_sem,
):
    depth, columns = coef_ref.shape
    units = columns // UNIT
    count = len(levels)

    places, partners = [], []
    for axis, bit, _ in levels:
        place = lax.axis_index(axis)
        upper = (place // 2**bit) % 2
        places.append(upper)
        partners.append({axis: place + (1 - 2 * upper) * 2**bit})
    outer = (places[1] + places[2] + 1) % 2
    hold = HOLD * outer
    dues = [inner + outer * (outside - inner) for _, _, (inner, outside) in levels]

    def cols(chunk):
        return pl.ds(pl.multiple_of(chunk * LANES, LANES), LANES)

    parts = [pl.ds(0, LANES), pl.ds(LANES, LANES), pl.ds(2 * LANES, columns - 2 * LANES)]

    def load_part(part):
        return pltpu.make_async_copy(
            coef_ref.at[:, parts[part]], stage.at[:, parts[part]], stage_sem.at[part]
        )

    def load_matrix(level):
        return pltpu.make_async_copy(transfer_ref.at[level], raw.at[level], raw_sem.at[level])

    later = pl.ds(2, count - 2)
    load_later = pltpu.make_async_copy(transfer_ref.at[later], raw.at[later], raw_sem.at[2])

    def send_first(part):
        return pltpu.make_async_remote_copy(
            src_ref=coef_ref.at[:, parts[part]],
            dst_ref=first.at[:, parts[part]],
            send_sem=first_send,
            recv_sem=first_recv.at[part],
            device_id=partners[0],
            device_id_type=pl.DeviceIdType.MESH,
        )

    def slot(unit):
        late = unit // (units - EDGE)
        early = 1 - (unit + units - EDGE) // units
        narrow = early + late
        return narrow * (unit - late * (units // 2 - EDGE)) + (1 - narrow) * (EDGE // 2 + unit // 2)

    def send(level, unit, rows):
        return pltpu.make_async_remote_copy(
            src_ref=mixed.at[level - 1, rows],
            dst_ref=landed.at[level - 1, rows],
            send_sem=send_sem,
            recv_sem=recv_sem.at[level - 1, slot(unit) % TURN],
            device_id=partners[level],
            device_id_type=pl.DeviceIdType.MESH,
        )

    load_limits = pltpu.make_async_copy(ranks_ref, limits, limits_sem)
    load_limits.start()
    load_matrix(0).start()
    load_part(0).start()
    barrier = pltpu.get_barrier_semaphore()
    for level in range(count):
        pl.semaphore_signal(
            barrier, inc=1, device_id=partners[level], device_id_type=pl.DeviceIdType.MESH
        )
    load_part(1).start()
    pl.semaphore_wait(barrier, count)
    for part in range(len(parts)):
        send_first(part).start()
    load_matrix(1).start()
    load_part(2).start()

    def prepare(level):
        if level < 2:
            load_matrix(level).wait()
        elif level == 2:
            load_later.wait()
        keep = lax.broadcasted_iota(jnp.int32, (depth, depth), 0) < limits[0, level]
        for side, place in enumerate((places[level], 1 - places[level])):
            block = raw[level, :, pl.ds(pl.multiple_of(place * depth, depth), depth)]
            both = split_rows(jnp.where(keep, block, jnp.zeros_like(block)).T)
            mats[level, 0, side * depth:(side + 1) * depth] = both[:depth]
            mats[level, 1, side * depth:(side + 1) * depth] = both[depth:]

    def mix(level, mine, other):
        total = None
        for part in range(2):
            for side, x in enumerate((mine, other)):
                term = jnp.dot(
                    x, mats[level, part, side * depth:(side + 1) * depth],
                    preferred_element_type=jnp.float32,
                )
                total = term if total is None else total + term
        half = total.shape[0] // 2
        return total[:half] + total[half:]

    def by_width(unit, body):
        inner = (unit >= EDGE) & (unit < units - EDGE)

        def run(start, width):
            start = pl.multiple_of(start, width)
            body(pl.ds(start, width), pl.ds(pl.multiple_of(2 * start, 2 * width), 2 * width))

        @pl.when(inner & (unit % 2 == 1))
        def _():
            run((unit - 1) * UNIT, 2 * UNIT)

        @pl.when(jnp.logical_not(inner))
        def _():
            run(unit * UNIT, UNIT)

    def spread(chunk, width):
        for source, target in ((stage, own), (first, given)):
            turned = source[:, cols(chunk)].T
            for start in range(0, LANES, width):
                where = pl.multiple_of(2 * (chunk * LANES + start), 2 * width)
                target[pl.ds(where, 2 * width)] = split_rows(turned[start:start + width])

    def open_chunk(chunk, width):
        for part in range(len(parts)):
            @pl.when(chunk == part)
            def _():
                load_part(part).wait()
                send_first(part).wait_recv()

        spread(chunk, width)

    def task_first(unit):
        inner = (unit >= EDGE) & (unit < units - EDGE)

        @pl.when(inner & (unit % EDGE == 1))
        def _():
            open_chunk(unit // EDGE, 2 * UNIT)

        @pl.when(jnp.logical_not(inner) & (unit % EDGE == 0))
        def _():
            open_chunk(unit // EDGE, UNIT)

        def body(rows, twice):
            result = mix(0, own[twice], given[twice])
            mixed[0, rows] = result
            own[twice] = split_rows(result)
            send(1, unit, rows).start()

        by_width(unit, body)

    def task(level, unit):
        def body(rows, twice):
            send(level, unit, rows).wait_recv()
            result = mix(level, own[twice], split_rows(landed[level - 1, rows]))
            if level + 1 < count:
                mixed[level, rows] = result
                own[twice] = split_rows(result)
                send(level + 1, unit, rows).start()
            else:
                done[rows] = result

        by_width(unit, body)
        if level + 1 == count:
            @pl.when(unit % EDGE == EDGE - 1)
            def _():
                chunk = unit // EDGE
                out_ref[:, cols(chunk)] = done[cols(chunk)].T

    load_limits.wait()
    prepare(0)

    def step(s, carry):
        @pl.when(s < units)
        def _():
            task_first(s)

        @pl.when(s == 0)
        def _():
            load_later.start()

        for level, due in enumerate(dues):
            if level == 1:
                at = s - due
                late = at // (units - HELD + hold)

                @pl.when((at >= 0) & (at < units + hold) & ((at < units - HELD) | (late > 0)))
                def _():
                    task(1, at - late * hold)

            elif level:
                @pl.when((s >= due) & (s < due + units))
                def _():
                    task(level, s - due)

            if level + 1 < count:
                @pl.when(s == due + 1)
                def _():
                    prepare(level + 1)
        return carry

    lax.fori_loop(0, dues[-1] + units, step, 0)

    pltpu.make_async_copy(mixed, mixed, send_sem).wait()
    pltpu.make_async_copy(coef_ref, coef_ref, first_send).wait()


def per_device(coefficients, transfer, ranks):
    levels = plan(
        lax.axis_size("node").bit_length() - 1, lax.axis_size("grp").bit_length() - 1
    )
    count = len(levels)
    depth, columns = coefficients.shape
    units = columns // UNIT
    call = pl.pallas_call(
        functools.partial(kernel, levels),
        out_shape=jax.ShapeDtypeStruct(coefficients.shape, jnp.float32),
        in_specs=[
            pl.BlockSpec(memory_space=pltpu.HBM),
            pl.BlockSpec(memory_space=pltpu.HBM),
            pl.BlockSpec(memory_space=pltpu.HBM),
        ],
        out_specs=pl.BlockSpec(memory_space=pltpu.VMEM),
        scratch_shapes=[
            pltpu.SMEM((1, count), jnp.int32),
            pltpu.VMEM((count, depth, 2 * depth), jnp.float32),
            pltpu.VMEM((count, 2, 2 * depth, depth), jnp.bfloat16),
            pltpu.VMEM((depth, columns), jnp.float32),
            pltpu.VMEM((depth, columns), jnp.float32),
            pltpu.VMEM((2 * columns, depth), jnp.bfloat16),
            pltpu.VMEM((2 * columns, depth), jnp.bfloat16),
            pltpu.VMEM((count - 1, columns, depth), jnp.float32),
            pltpu.VMEM((count - 1, columns, depth), jnp.float32),
            pltpu.VMEM((columns, depth), jnp.float32),
            pltpu.SemaphoreType.DMA,
            pltpu.SemaphoreType.DMA((3,)),
            pltpu.SemaphoreType.DMA((3,)),
            pltpu.SemaphoreType.DMA,
            pltpu.SemaphoreType.DMA((3,)),
            pltpu.SemaphoreType.DMA,
            pltpu.SemaphoreType.DMA((count - 1, TURN)),
        ],
        compiler_params=pltpu.CompilerParams(
            collective_id=0, has_side_effects=True, vmem_limit_bytes=55_000_000
        ),
        name="butterfly",
    )
    return call(pltpu.with_memory_space_constraint(ranks.T, pltpu.HBM), coefficients, transfer)


def solution(mesh):
    return jax.shard_map(
        per_device,
        mesh=mesh,
        in_specs=(
            P(("grp", "node"), None),
            P(None, ("grp", "node"), None),
            P(None, ("grp", "node")),
        ),
        out_specs=P(("grp", "node"), None),
        check_vma=False,
    )
```

```python
import functools

import jax
import jax.numpy as jnp
from jax import lax
from jax.experimental import pallas as pl
from jax.experimental.pallas import tpu as pltpu
from jax.sharding import PartitionSpec as P

LANES = 128
UNIT = 32
EDGE = LANES // UNIT
HELD, HOLD = 3, 3
TURN = 10
LAGS = ((4, 6, 4), (6, 4, 4))


def split_rows(x):
    high = x.astype(jnp.bfloat16)
    low = (x - high.astype(jnp.float32)).astype(jnp.bfloat16)
    return jnp.concatenate([high, low], axis=0)


def plan(node_bits, group_bits):
    levels, due = [], (0, 0)
    for bit in range(node_bits):
        if bit:
            due = tuple(d + lag[min(bit, 2) - 1] for d, lag in zip(due, LAGS))
        levels.append(("node", bit, due))
    for bit in range(group_bits):
        due = tuple(d + lag[2] for d, lag in zip(due, LAGS))
        levels.append(("grp", bit, due))
    return levels


def kernel(
    levels, ranks_ref, coef_ref, transfer_ref, out_ref,
    limits, raw, mats, stage, first, own, given, landed, mixed, done,
    limits_sem, raw_sem, stage_sem, first_send, first_recv, send_sem, recv_sem,
):
    depth, columns = coef_ref.shape
    units = columns // UNIT
    count = len(levels)

    places, partners = [], []
    for axis, bit, _ in levels:
        place = lax.axis_index(axis)
        upper = (place // 2**bit) % 2
        places.append(upper)
        partners.append({axis: place + (1 - 2 * upper) * 2**bit})
    outer = (places[1] + places[2] + 1) % 2
    hold = HOLD * outer
    dues = [inner + outer * (outside - inner) for _, _, (inner, outside) in levels]

    def cols(chunk):
        return pl.ds(pl.multiple_of(chunk * LANES, LANES), LANES)

    parts = [pl.ds(0, LANES), pl.ds(LANES, LANES), pl.ds(2 * LANES, columns - 2 * LANES)]

    def load_part(part):
        return pltpu.make_async_copy(
            coef_ref.at[:, parts[part]], stage.at[:, parts[part]], stage_sem.at[part]
        )

    def load_matrix(level):
        return pltpu.make_async_copy(transfer_ref.at[level], raw.at[level], raw_sem.at[level])

    later = pl.ds(2, count - 2)
    load_later = pltpu.make_async_copy(transfer_ref.at[later], raw.at[later], raw_sem.at[2])

    def send_first(part):
        return pltpu.make_async_remote_copy(
            src_ref=coef_ref.at[:, parts[part]],
            dst_ref=first.at[:, parts[part]],
            send_sem=first_send,
            recv_sem=first_recv.at[part],
            device_id=partners[0],
            device_id_type=pl.DeviceIdType.MESH,
        )

    def slot(unit):
        late = unit // (units - EDGE)
        early = 1 - (unit + units - EDGE) // units
        narrow = early + late
        return narrow * (unit - late * (units // 2 - EDGE)) + (1 - narrow) * (EDGE // 2 + unit // 2)

    def send(level, unit, rows):
        return pltpu.make_async_remote_copy(
            src_ref=mixed.at[level - 1, rows],
            dst_ref=landed.at[level - 1, rows],
            send_sem=send_sem,
            recv_sem=recv_sem.at[level - 1, slot(unit) % TURN],
            device_id=partners[level],
            device_id_type=pl.DeviceIdType.MESH,
        )

    load_limits = pltpu.make_async_copy(ranks_ref, limits, limits_sem)
    load_limits.start()
    load_matrix(0).start()
    load_part(0).start()
    barrier = pltpu.get_barrier_semaphore()
    for level in range(count):
        pl.semaphore_signal(
            barrier, inc=1, device_id=partners[level], device_id_type=pl.DeviceIdType.MESH
        )
    load_part(1).start()
    pl.semaphore_wait(barrier, count)
    for part in range(2):
        send_first(part).start()
    load_matrix(1).start()

    def prepare(level):
        if level < 2:
            load_matrix(level).wait()
        elif level == 2:
            load_later.wait()
        keep = lax.broadcasted_iota(jnp.int32, (depth, depth), 0) < limits[0, level]
        for side, place in enumerate((places[level], 1 - places[level])):
            block = raw[level, :, pl.ds(pl.multiple_of(place * depth, depth), depth)]
            both = split_rows(jnp.where(keep, block, jnp.zeros_like(block)).T)
            mats[level, 0, side * depth:(side + 1) * depth] = both[:depth]
            mats[level, 1, side * depth:(side + 1) * depth] = both[depth:]

    def mix(level, mine, other):
        total = None
        for part in range(2):
            for side, x in enumerate((mine, other)):
                term = jnp.dot(
                    x, mats[level, part, side * depth:(side + 1) * depth],
                    preferred_element_type=jnp.float32,
                )
                total = term if total is None else total + term
        half = total.shape[0] // 2
        return total[:half] + total[half:]

    def by_width(unit, body):
        inner = (unit >= EDGE) & (unit < units - EDGE)

        def run(start, width):
            start = pl.multiple_of(start, width)
            body(pl.ds(start, width), pl.ds(pl.multiple_of(2 * start, 2 * width), 2 * width))

        @pl.when(inner & (unit % 2 == 1))
        def _():
            run((unit - 1) * UNIT, 2 * UNIT)

        @pl.when(jnp.logical_not(inner))
        def _():
            run(unit * UNIT, UNIT)

    def spread(chunk, width):
        for source, target in ((stage, own), (first, given)):
            turned = source[:, cols(chunk)].T
            for start in range(0, LANES, width):
                where = pl.multiple_of(2 * (chunk * LANES + start), 2 * width)
                target[pl.ds(where, 2 * width)] = split_rows(turned[start:start + width])

    def open_chunk(chunk, width):
        for part in range(len(parts)):
            @pl.when(chunk == part)
            def _():
                load_part(part).wait()
                send_first(part).wait_recv()

        spread(chunk, width)

    def task_first(unit):
        inner = (unit >= EDGE) & (unit < units - EDGE)

        @pl.when(inner & (unit % EDGE == 1))
        def _():
            open_chunk(unit // EDGE, 2 * UNIT)

        @pl.when(jnp.logical_not(inner) & (unit % EDGE == 0))
        def _():
            open_chunk(unit // EDGE, UNIT)

        def body(rows, twice):
            result = mix(0, own[twice], given[twice])
            mixed[0, rows] = result
            own[twice] = split_rows(result)
            send(1, unit, rows).start()

        by_width(unit, body)

    def task(level, unit):
        def body(rows, twice):
            send(level, unit, rows).wait_recv()
            result = mix(level, own[twice], split_rows(landed[level - 1, rows]))
            if level + 1 < count:
                mixed[level, rows] = result
                own[twice] = split_rows(result)
                send(level + 1, unit, rows).start()
            else:
                done[rows] = result

        by_width(unit, body)
        if level + 1 == count:
            @pl.when(unit % EDGE == EDGE - 1)
            def _():
                chunk = unit // EDGE
                out_ref[:, cols(chunk)] = done[cols(chunk)].T

    load_limits.wait()
    prepare(0)

    def step(s, carry):
        @pl.when(s < units)
        def _():
            task_first(s)

        @pl.when(s == 0)
        def _():
            send_first(2).start()
            load_part(2).start()
            load_later.start()

        for level, due in enumerate(dues):
            if level == 1:
                at = s - due
                late = at // (units - HELD + hold)

                @pl.when((at >= 0) & (at < units + hold) & ((at < units - HELD) | (late > 0)))
                def _():
                    task(1, at - late * hold)

            elif level:
                @pl.when((s >= due) & (s < due + units))
                def _():
                    task(level, s - due)

            if level + 1 < count:
                @pl.when(s == due + 1)
                def _():
                    prepare(level + 1)
        return carry

    lax.fori_loop(0, dues[-1] + units, step, 0)

    pltpu.make_async_copy(mixed, mixed, send_sem).wait()
    pltpu.make_async_copy(coef_ref, coef_ref, first_send).wait()


def per_device(coefficients, transfer, ranks):
    levels = plan(
        lax.axis_size("node").bit_length() - 1, lax.axis_size("grp").bit_length() - 1
    )
    count = len(levels)
    depth, columns = coefficients.shape
    units = columns // UNIT
    call = pl.pallas_call(
        functools.partial(kernel, levels),
        out_shape=jax.ShapeDtypeStruct(coefficients.shape, jnp.float32),
        in_specs=[
            pl.BlockSpec(memory_space=pltpu.HBM),
            pl.BlockSpec(memory_space=pltpu.HBM),
            pl.BlockSpec(memory_space=pltpu.HBM),
        ],
        out_specs=pl.BlockSpec(memory_space=pltpu.VMEM),
        scratch_shapes=[
            pltpu.SMEM((1, count), jnp.int32),
            pltpu.VMEM((count, depth, 2 * depth), jnp.float32),
            pltpu.VMEM((count, 2, 2 * depth, depth), jnp.bfloat16),
            pltpu.VMEM((depth, columns), jnp.float32),
            pltpu.VMEM((depth, columns), jnp.float32),
            pltpu.VMEM((2 * columns, depth), jnp.bfloat16),
            pltpu.VMEM((2 * columns, depth), jnp.bfloat16),
            pltpu.VMEM((count - 1, columns, depth), jnp.float32),
            pltpu.VMEM((count - 1, columns, depth), jnp.float32),
            pltpu.VMEM((columns, depth), jnp.float32),
            pltpu.SemaphoreType.DMA,
            pltpu.SemaphoreType.DMA((3,)),
            pltpu.SemaphoreType.DMA((3,)),
            pltpu.SemaphoreType.DMA,
            pltpu.SemaphoreType.DMA((3,)),
            pltpu.SemaphoreType.DMA,
            pltpu.SemaphoreType.DMA((count - 1, TURN)),
        ],
        compiler_params=pltpu.CompilerParams(
            collective_id=0, has_side_effects=True, vmem_limit_bytes=55_000_000
        ),
        name="butterfly",
    )
    return call(pltpu.with_memory_space_constraint(ranks.T, pltpu.HBM), coefficients, transfer)


def solution(mesh):
    return jax.shard_map(
        per_device,
        mesh=mesh,
        in_specs=(
            P(("grp", "node"), None),
            P(None, ("grp", "node"), None),
            P(None, ("grp", "node")),
        ),
        out_specs=P(("grp", "node"), None),
        check_vma=False,
    )
```

```python
import functools

import jax
import jax.numpy as jnp
from jax import lax
from jax.experimental import pallas as pl
from jax.experimental.pallas import tpu as pltpu
from jax.sharding import PartitionSpec as P

LANES = 128
UNIT = 32
EDGE = LANES // UNIT
HELD, HOLD = 3, 3
TURN = 10
LAGS = ((4, 6, 4), (6, 4, 4))


def split_rows(x):
    high = x.astype(jnp.bfloat16)
    low = (x - high.astype(jnp.float32)).astype(jnp.bfloat16)
    return jnp.concatenate([high, low], axis=0)


def plan(node_bits, group_bits):
    levels, due = [], (0, 0)
    for bit in range(node_bits):
        if bit:
            due = tuple(d + lag[min(bit, 2) - 1] for d, lag in zip(due, LAGS))
        levels.append(("node", bit, due))
    for bit in range(group_bits):
        due = tuple(d + lag[2] for d, lag in zip(due, LAGS))
        levels.append(("grp", bit, due))
    return levels


def kernel(
    levels, ranks_ref, coef_ref, transfer_ref, out_ref,
    limits, raw, mats, stage, first, own, given, landed, mixed, done,
    limits_sem, raw_sem, stage_sem, first_send, first_recv, send_sem, recv_sem,
):
    depth, columns = coef_ref.shape
    units = columns // UNIT
    count = len(levels)

    places, partners = [], []
    for axis, bit, _ in levels:
        place = lax.axis_index(axis)
        upper = (place // 2**bit) % 2
        places.append(upper)
        partners.append({axis: place + (1 - 2 * upper) * 2**bit})
    outer = (places[1] + places[2] + 1) % 2
    hold = HOLD * outer + (1 - outer) * places[0]
    dues = [inner + outer * (outside - inner) for _, _, (inner, outside) in levels]

    def cols(chunk):
        return pl.ds(pl.multiple_of(chunk * LANES, LANES), LANES)

    parts = [pl.ds(0, LANES), pl.ds(LANES, LANES), pl.ds(2 * LANES, columns - 2 * LANES)]

    def load_part(part):
        return pltpu.make_async_copy(
            coef_ref.at[:, parts[part]], stage.at[:, parts[part]], stage_sem.at[part]
        )

    def load_matrix(level):
        return pltpu.make_async_copy(transfer_ref.at[level], raw.at[level], raw_sem.at[level])

    later = pl.ds(2, count - 2)
    load_later = pltpu.make_async_copy(transfer_ref.at[later], raw.at[later], raw_sem.at[2])

    def send_first(part):
        return pltpu.make_async_remote_copy(
            src_ref=coef_ref.at[:, parts[part]],
            dst_ref=first.at[:, parts[part]],
            send_sem=first_send,
            recv_sem=first_recv.at[part],
            device_id=partners[0],
            device_id_type=pl.DeviceIdType.MESH,
        )

    def slot(unit):
        late = unit // (units - EDGE)
        early = 1 - (unit + units - EDGE) // units
        narrow = early + late
        return narrow * (unit - late * (units // 2 - EDGE)) + (1 - narrow) * (EDGE // 2 + unit // 2)

    def send(level, unit, rows):
        return pltpu.make_async_remote_copy(
            src_ref=mixed.at[level - 1, rows],
            dst_ref=landed.at[level - 1, rows],
            send_sem=send_sem,
            recv_sem=recv_sem.at[level - 1, slot(unit) % TURN],
            device_id=partners[level],
            device_id_type=pl.DeviceIdType.MESH,
        )

    load_limits = pltpu.make_async_copy(ranks_ref, limits, limits_sem)
    load_limits.start()
    load_matrix(0).start()
    load_part(0).start()
    barrier = pltpu.get_barrier_semaphore()
    for level in range(count):
        pl.semaphore_signal(
            barrier, inc=1, device_id=partners[level], device_id_type=pl.DeviceIdType.MESH
        )
    load_part(1).start()
    pl.semaphore_wait(barrier, count)
    for part in range(2):
        send_first(part).start()
    load_matrix(1).start()

    def prepare(level):
        if level < 2:
            load_matrix(level).wait()
        elif level == 2:
            load_later.wait()
        keep = lax.broadcasted_iota(jnp.int32, (depth, depth), 0) < limits[0, level]
        for side, place in enumerate((places[level], 1 - places[level])):
            block = raw[level, :, pl.ds(pl.multiple_of(place * depth, depth), depth)]
            both = split_rows(jnp.where(keep, block, jnp.zeros_like(block)).T)
            mats[level, 0, side * depth:(side + 1) * depth] = both[:depth]
            mats[level, 1, side * depth:(side + 1) * depth] = both[depth:]

    def mix(level, mine, other):
        total = None
        for part in range(2):
            for side, x in enumerate((mine, other)):
                term = jnp.dot(
                    x, mats[level, part, side * depth:(side + 1) * depth],
                    preferred_element_type=jnp.float32,
                )
                total = term if total is None else total + term
        half = total.shape[0] // 2
        return total[:half] + total[half:]

    def by_width(unit, body):
        inner = (unit >= EDGE) & (unit < units - EDGE)

        def run(start, width):
            start = pl.multiple_of(start, width)
            body(pl.ds(start, width), pl.ds(pl.multiple_of(2 * start, 2 * width), 2 * width))

        @pl.when(inner & (unit % 2 == 1))
        def _():
            run((unit - 1) * UNIT, 2 * UNIT)

        @pl.when(jnp.logical_not(inner))
        def _():
            run(unit * UNIT, UNIT)

    def spread(chunk, width):
        for source, target in ((stage, own), (first, given)):
            turned = source[:, cols(chunk)].T
            for start in range(0, LANES, width):
                where = pl.multiple_of(2 * (chunk * LANES + start), 2 * width)
                target[pl.ds(where, 2 * width)] = split_rows(turned[start:start + width])

    def open_chunk(chunk, width):
        for part in range(len(parts)):
            @pl.when(chunk == part)
            def _():
                load_part(part).wait()
                send_first(part).wait_recv()

        spread(chunk, width)

    def task_first(unit):
        inner = (unit >= EDGE) & (unit < units - EDGE)

        @pl.when(inner & (unit % EDGE == 1))
        def _():
            open_chunk(unit // EDGE, 2 * UNIT)

        @pl.when(jnp.logical_not(inner) & (unit % EDGE == 0))
        def _():
            open_chunk(unit // EDGE, UNIT)

        def body(rows, twice):
            result = mix(0, own[twice], given[twice])
            mixed[0, rows] = result
            own[twice] = split_rows(result)
            send(1, unit, rows).start()

        by_width(unit, body)

    def task(level, unit):
        def body(rows, twice):
            send(level, unit, rows).wait_recv()
            result = mix(level, own[twice], split_rows(landed[level - 1, rows]))
            if level + 1 < count:
                mixed[level, rows] = result
                own[twice] = split_rows(result)
                send(level + 1, unit, rows).start()
            else:
                done[rows] = result

        by_width(unit, body)
        if level + 1 == count:
            @pl.when(unit % EDGE == EDGE - 1)
            def _():
                chunk = unit // EDGE
                out_ref[:, cols(chunk)] = done[cols(chunk)].T

    load_limits.wait()
    prepare(0)

    def step(s, carry):
        @pl.when(s < units)
        def _():
            task_first(s)

        @pl.when(s == 0)
        def _():
            send_first(2).start()
            load_part(2).start()
            load_later.start()

        for level, due in enumerate(dues):
            if level == 1:
                at = s - due
                late = at // (units - HELD + hold)

                @pl.when((at >= 0) & (at < units + hold) & ((at < units - HELD) | (late > 0)))
                def _():
                    task(1, at - late * hold)

            elif level:
                @pl.when((s >= due) & (s < due + units))
                def _():
                    task(level, s - due)

            if level + 1 < count:
                @pl.when(s == due + 1)
                def _():
                    prepare(level + 1)
        return carry

    lax.fori_loop(0, dues[-1] + units, step, 0)

    pltpu.make_async_copy(mixed, mixed, send_sem).wait()
    pltpu.make_async_copy(coef_ref, coef_ref, first_send).wait()


def per_device(coefficients, transfer, ranks):
    levels = plan(
        lax.axis_size("node").bit_length() - 1, lax.axis_size("grp").bit_length() - 1
    )
    count = len(levels)
    depth, columns = coefficients.shape
    units = columns // UNIT
    call = pl.pallas_call(
        functools.partial(kernel, levels),
        out_shape=jax.ShapeDtypeStruct(coefficients.shape, jnp.float32),
        in_specs=[
            pl.BlockSpec(memory_space=pltpu.HBM),
            pl.BlockSpec(memory_space=pltpu.HBM),
            pl.BlockSpec(memory_space=pltpu.HBM),
        ],
        out_specs=pl.BlockSpec(memory_space=pltpu.VMEM),
        scratch_shapes=[
            pltpu.SMEM((1, count), jnp.int32),
            pltpu.VMEM((count, depth, 2 * depth), jnp.float32),
            pltpu.VMEM((count, 2, 2 * depth, depth), jnp.bfloat16),
            pltpu.VMEM((depth, columns), jnp.float32),
            pltpu.VMEM((depth, columns), jnp.float32),
            pltpu.VMEM((2 * columns, depth), jnp.bfloat16),
            pltpu.VMEM((2 * columns, depth), jnp.bfloat16),
            pltpu.VMEM((count - 1, columns, depth), jnp.float32),
            pltpu.VMEM((count - 1, columns, depth), jnp.float32),
            pltpu.VMEM((columns, depth), jnp.float32),
            pltpu.SemaphoreType.DMA,
            pltpu.SemaphoreType.DMA((3,)),
            pltpu.SemaphoreType.DMA((3,)),
            pltpu.SemaphoreType.DMA,
            pltpu.SemaphoreType.DMA((3,)),
            pltpu.SemaphoreType.DMA,
            pltpu.SemaphoreType.DMA((count - 1, TURN)),
        ],
        compiler_params=pltpu.CompilerParams(
            collective_id=0, has_side_effects=True, vmem_limit_bytes=55_000_000
        ),
        name="butterfly",
    )
    return call(pltpu.with_memory_space_constraint(ranks.T, pltpu.HBM), coefficients, transfer)


def solution(mesh):
    return jax.shard_map(
        per_device,
        mesh=mesh,
        in_specs=(
            P(("grp", "node"), None),
            P(None, ("grp", "node"), None),
            P(None, ("grp", "node")),
        ),
        out_specs=P(("grp", "node"), None),
        check_vma=False,
    )
```
